256 devices in a mesh: dp: 16 (over z, y_hi), row: 4 (over y_lo, core), col: 4 (over x).
Axes of the slice: x: 4, y: 4 (y_hi: 2, y_lo: 2; y = y_hi * 2 + y_lo), z: 8, core: 2. Of those that a mesh axis runs over, the one named last changes fastest.
Arguments:
- tokens: bfloat16 [7168, 4096], P(('dp', 'col'), 'row'), may hold values from -6 to 6
- gate_up: bfloat16 [2, 4096, 14336], P(None, 'row', ('dp', 'col')), may hold values from -0.09375 to 0.09375
- down_weight: bfloat16 [14336, 4096], P(('dp', 'col'), 'row'), may hold values from -0.046875 to 0.046875
Outputs:
- mixed: bfloat16 [7168, 4096], P(('dp', 'col'), 'row')
- col_check: float32 [4096], P('row')
- row_check: float32 [7168], P(('dp', 'col'))
The draws below stay inside these ranges and needn't reach their ends.
All inputs are finite; a program needn't handle non-finite values.
Results may differ from the reference program's by a relative error of at most 0.0049.
Values may be sent and summed in bfloat16 or wider, within the bound.
No kernel may reach another device: no remote copies, remote signals or barrier semaphores. Data moves between devices by JAX's collectives and lax.ppermute only.
A program may use at most 128 MiB of HBM per device.

```python
import math
import jax
import jax.numpy as jnp
from jax import lax

D = 4096
FF = 14336
TOKENS = 7168


def shard_levels(stream_key, dims, shards, least, top_value):
    gain = 1.0
    for dim, shards_of in shards:
        draws = jax.random.uniform(jax.random.fold_in(jax.random.fold_in(stream_key, 6), dim), (shards_of,), jnp.float32, least / len(shards), top_value / len(shards))
        gain = gain * jnp.repeat(jnp.exp(draws), dims[dim] // shards_of).reshape((-1,) + (1,) * (len(dims) - 1 - dim))
    return gain


def gaussian(own_key, extent, width, reach, cuts=(), dtype=jnp.bfloat16):
    array = jax.random.normal(own_key, extent, jnp.float32) * width
    if len(cuts) > 0:
        array = shard_levels(own_key, extent, cuts, -0.22, 0.18) * array
    return jnp.clip(array, min=-reach, max=reach).astype(dtype)


def setup_inputs(seed: int = 0) -> dict:
    keys = jax.random.split(jax.random.key(seed), 4)
    tokens = gaussian(keys[0], (TOKENS, D), 1.0, 6.0, ((0, 64), (1, 4)))
    gate_up = gaussian(keys[1], (2, D, FF), D ** -0.5, 0.09375, ((1, 4), (2, 64)))
    down_weight = gaussian(keys[2], (FF, D), FF ** -0.5, 0.046875, ((0, 64), (1, 4)))
    return dict(tokens=tokens, gate_up=gate_up, down_weight=down_weight)


def reference(tokens, gate_up, down_weight):
    gate = jnp.dot(tokens, gate_up[0], preferred_element_type=jnp.float32)
    up = jnp.dot(tokens, gate_up[1], preferred_element_type=jnp.float32)
    hidden = (jax.nn.silu(gate) * up).astype(jnp.bfloat16)
    mixed = jnp.dot(hidden, down_weight, preferred_element_type=jnp.float32).astype(jnp.bfloat16)
    hidden_wide = hidden.astype(jnp.float32)
    weight_wide = down_weight.astype(jnp.float32)
    unit_sums = lax.optimization_barrier(jnp.sum(hidden_wide, axis=0))
    col_check = jnp.dot(unit_sums, weight_wide, precision=lax.Precision.HIGHEST) / math.sqrt(TOKENS)
    weight_sums = lax.optimization_barrier(jnp.sum(weight_wide, axis=1))
    row_check = jnp.dot(hidden_wide, weight_sums, precision=lax.Precision.HIGHEST) / math.sqrt(D)
    return (mixed, col_check, row_check)
```

```python
import math

import jax
import jax.numpy as jnp
import numpy as np
from jax import lax
from jax.sharding import Mesh, PartitionSpec as P

ROW = ("yl", "c")
Y = ("yh", "yl")


def ring(n, step):
    return [(i, (i - step) % n) for i in range(n)]


def flip(n, mask):
    return [(i, i ^ mask) for i in range(n)]


def split(value):
    high = lax.reduce_precision(value, 8, 7)
    return high.astype(jnp.bfloat16), (value - high).astype(jnp.bfloat16)


def swiglu(gate, up):
    return (jax.nn.silu(gate) * up).astype(jnp.bfloat16)


def sum_over(value, axis, n):
    mask = 1
    while mask < n:
        value = value + lax.ppermute(value, axis, flip(n, mask))
        mask *= 2
    return value


def per_device(tokens, gate_up, down_weight):
    rows, width = tokens.shape
    units = gate_up.shape[2]
    nz, nx, nyh, nrow = (lax.axis_size(a) for a in ("z", "x", "yh", ROW))
    part = units // nrow
    total_tokens = rows * nz * nx * nyh
    model_width = width * nrow
    own = lax.axis_index(ROW)

    pieces = jnp.swapaxes(gate_up, 1, 2).reshape(2, nrow, part, width)
    weights = []
    for k in range(nrow):
        piece = lax.dynamic_index_in_dim(pieces, own ^ k, 1, keepdims=False)
        weights.append(piece if k == 0 else lax.ppermute(piece, ROW, flip(nrow, k)))
    weights = jnp.concatenate(weights, axis=-1)
    weights = lax.all_gather(weights, "z", axis=0, tiled=False)

    sums = jnp.sum(down_weight.astype(jnp.float32), axis=1)
    sums = sum_over(sum_over(sums, "c", 2), "yl", 2)
    down = down_weight.reshape(nrow, part, width)
    order = [own ^ k for k in range(nrow)]
    down = jnp.concatenate([lax.dynamic_slice_in_dim(down, q, 1, 0) for q in order])
    sums = jnp.concatenate(
        [lax.dynamic_slice_in_dim(sums.reshape(nrow, part), q, 1, 0) for q in order]
    )
    down = lax.all_gather(down, "z", axis=0, tiled=False)
    sums = lax.all_gather(sums, "z", axis=0, tiled=False)

    group = jnp.concatenate(
        [tokens] + [lax.ppermute(tokens, "x", ring(nx, k)) for k in range(1, nx)]
    )
    group = [group] + [lax.ppermute(group, Y, flip(2 * nyh, k)) for k in range(1, 2 * nyh)]
    mine = [jnp.concatenate([group[d], group[2 + d]]) for d in (0, 1)]
    other = [lax.ppermute(m, "c", flip(2, 1)) for m in mine]
    wide = jnp.concatenate([mine[0], other[0], mine[1], other[1]], axis=-1)

    gate_up_sum = jnp.einsum("td,zgfd->tgzf", wide, weights, preferred_element_type=jnp.float32)
    hidden = swiglu(gate_up_sum[:, 0], gate_up_sum[:, 1])
    far = lax.ppermute(hidden, "yl", flip(2, 1))
    hidden = [hidden, lax.ppermute(hidden, "c", flip(2, 1)), far, lax.ppermute(far, "c", flip(2, 1))]
    hidden = jnp.stack(hidden, axis=2)
    hidden_wide = hidden.astype(jnp.float32)

    unit_sums = sum_over(jnp.sum(hidden_wide, axis=0), "z", nz)
    out = jnp.einsum("tzkf,zkfd->td", hidden, down, preferred_element_type=jnp.float32)
    col = jnp.einsum(
        "zkf,zkfd->d", unit_sums, down.astype(jnp.float32), precision=lax.Precision.HIGHEST
    )
    row = jnp.einsum("tzkf,zkf->t", hidden_wide, sums, precision=lax.Precision.HIGHEST)

    out = out.reshape(nyh, nx, rows, width)
    row = row.reshape(nyh, nx, rows)
    received = []
    for dy in range(nyh):
        for dx in range(nx):
            row_pad = jnp.pad(row[dy, dx], (0, width - rows))
            extra = jnp.stack([*split(col), *split(row_pad)])
            extra = jnp.pad(extra, ((0, 4), (0, 0)))
            sent = jnp.concatenate([out[dy, dx].astype(jnp.bfloat16), extra])
            if dx or dy:
                perm = [
                    (h * nx + i, (h ^ dy) * nx + (i + dx) % nx)
                    for h in range(nyh)
                    for i in range(nx)
                ]
                sent = lax.ppermute(sent, ("yh", "x"), perm)
            received.append(sent.astype(jnp.float32))
    result = sum(received)
    mixed = result[:rows].astype(jnp.bfloat16)
    col_check = (result[rows] + result[rows + 1]) / math.sqrt(total_tokens)
    row_check = (result[rows + 2] + result[rows + 3])[:rows] / math.sqrt(model_width)
    return (mixed, col_check, row_check)


def solution(mesh):
    shape = mesh.shape
    devices = np.asarray(mesh.devices).reshape(shape["dp"] // 2, 2, shape["row"] // 2, 2, shape["col"])
    fine = Mesh(devices, ("z", "yh", "yl", "c", "x"))
    batch, wide = ("z", "yh", "x"), ("yl", "c")
    return jax.shard_map(
        per_device,
        mesh=fine,
        in_specs=(P(batch, wide), P(None, wide, batch), P(batch, wide)),
        out_specs=(P(batch, wide), P(wide), P(batch)),
        check_vma=False,
    )
```

```python
import functools
import math

import jax
import jax.numpy as jnp
import numpy as np
from jax import lax
from jax.experimental import pallas as pl
from jax.experimental.pallas import tpu as pltpu
from jax.sharding import Mesh, PartitionSpec as P

ROW = ("yl", "c")
EXTRA = 8
MINOR = (((1,), (1,)), ((), ()))
MAJOR = (((0,), (0,)), ((), ()))
F32 = jnp.float32
BF16 = jnp.bfloat16


def shift(n, step):
    return [(i, (i + step) % n) for i in range(n)]


def flip(n, mask):
    return [(i, i ^ mask) for i in range(n)]


def sum_over(value, axis, n):
    mask = 1
    while mask < n:
        value = value + lax.ppermute(value, axis, flip(n, mask))
        mask *= 2
    return value


def hidden_kernel(*refs):
    x_refs, weights_ref, out_ref = refs[:8], refs[8], refs[9]
    count, part = out_ref.shape[:2]
    depth = x_refs[0].shape[1]
    total = None
    for k in range(4):
        near = 4 * (k % 2) + k // 2
        x = jnp.concatenate([x_refs[near][...], x_refs[near + 2][...]])
        weights = weights_ref[:, pl.ds(k * depth, depth)]
        product = lax.dot_general(weights, x, MINOR, preferred_element_type=F32)
        total = product if total is None else total + product
    for j in range(count):
        gate = total[2 * part * j : 2 * part * j + part]
        up = total[2 * part * j + part : 2 * part * (j + 1)]
        out_ref[j] = (gate / (1.0 + jnp.exp(-gate)) * up).astype(BF16)


def hidden_units(mine, other, weights):
    count, units, wide = weights.shape
    total = 2 * mine[0].shape[0]
    return pl.pallas_call(
        hidden_kernel,
        out_shape=jax.ShapeDtypeStruct((count, units // 2, total), BF16),
        compiler_params=pltpu.CompilerParams(vmem_limit_bytes=56 << 20),
        cost_estimate=pl.CostEstimate(
            flops=2 * count * units * total * wide,
            transcendentals=count * units * total // 2,
            bytes_accessed=2 * (total + count * units) * wide,
        ),
        name="hidden",
    )(*mine, *other, weights.reshape(count * units, wide))


def output_kernel(pieces, blocks, *refs):
    hidden_refs, (down_ref, units_ref, weights_ref) = refs[:pieces], refs[pieces : pieces + 3]
    out_refs, (total, col, row) = refs[pieces + 3 : -3], refs[-3:]
    units = sum(r.shape[0] for r in hidden_refs)
    width = down_ref.shape[1]
    rows = total.shape[0] // blocks

    @pl.when(pl.program_id(0) == 0)
    def _():
        for sums in (total, col, row):
            sums[...] = jnp.zeros_like(sums)

    def fold(value):
        return jnp.sum(value.reshape(units // 8, 8, value.shape[1]), axis=0)

    hidden = jnp.concatenate([r[...].astype(F32) for r in hidden_refs])
    down = down_ref[pl.ds(0, units), :]
    total[...] += lax.dot_general(hidden.astype(BF16), down, MAJOR, preferred_element_type=F32)
    col[...] += fold(units_ref[...] * down.astype(F32))
    row[...] += fold(weights_ref[...] * hidden)

    @pl.when(pl.program_id(0) == pl.num_programs(0) - 1)
    def _():
        lines = []
        for sums in (col, row):
            value = jnp.sum(sums[...], axis=0, keepdims=True)
            high = value.astype(BF16).astype(F32)
            for line in (high, value - high):
                short = width - line.shape[1]
                if short:
                    line = jnp.concatenate([line, jnp.zeros((1, short), F32)], axis=1)
                lines.append(line)
        lines.append(jnp.zeros((EXTRA - len(lines), width), F32))
        lines = jnp.concatenate(lines).astype(BF16)
        for j in range(blocks):
            out_refs[j][pl.ds(0, rows), :] = total[pl.ds(j * rows, rows), :].astype(BF16)
            out_refs[j][pl.ds(rows, EXTRA), :] = lines


def outputs(hidden, down, unit_sums, weight_sums, blocks):
    steps, _, total = hidden[0].shape
    units = sum(h.shape[1] for h in hidden)
    width = down.shape[2]
    operands = [*hidden, down, unit_sums, weight_sums]
    piece = (total // blocks + EXTRA, width)
    return pl.pallas_call(
        functools.partial(output_kernel, len(hidden), blocks),
        out_shape=[jax.ShapeDtypeStruct(piece, BF16)] * blocks,
        grid=(steps,),
        in_specs=[pl.BlockSpec((None, *a.shape[1:]), lambda s: (s, 0, 0)) for a in operands],
        out_specs=[pl.BlockSpec(piece, lambda s: (0, 0))] * blocks,
        scratch_shapes=[
            pltpu.VMEM((total, width), F32),
            pltpu.VMEM((8, width), F32),
            pltpu.VMEM((8, total), F32),
        ],
        compiler_params=pltpu.CompilerParams(vmem_limit_bytes=48 << 20),
        cost_estimate=pl.CostEstimate(
            flops=2 * steps * units * total * width,
            transcendentals=0,
            bytes_accessed=2 * steps * units * (total + width) + 2 * total * width,
        ),
        name="outputs",
    )(*operands)


def per_device(tokens, gate_up, down_weight):
    rows, width = tokens.shape
    units = gate_up.shape[2]
    nz, nx, nyh, nyl, nrow = (lax.axis_size(a) for a in ("z", "x", "yh", "yl", ROW))
    part = units // nrow
    total_tokens = rows * nz * nx * nyh
    model_width = width * nrow
    own = lax.axis_index(ROW)

    def across(array, mask):
        return lax.ppermute(array, ("yh", "yl"), flip(nyh * nyl, mask))

    def swap(array):
        return lax.ppermute(array, "c", flip(2, 1))

    pieces = jnp.swapaxes(gate_up, 1, 2).reshape(2, nrow, part, width)
    weights = []
    for k in range(nrow):
        piece = lax.dynamic_index_in_dim(pieces, own ^ k, 1, keepdims=False)
        piece = piece.reshape(2 * part, width)
        weights.append(piece if k == 0 else lax.ppermute(piece, ROW, flip(nrow, k)))
    weights = lax.all_gather(jnp.concatenate(weights, axis=1), "z", axis=0, tiled=False)

    def ordered(array):
        array = array.reshape(nrow, part, -1)
        array = jnp.concatenate(
            [lax.dynamic_slice_in_dim(array, own ^ k, 1, 0) for k in range(nrow)]
        )
        return array.reshape(units, -1)

    sums = jnp.sum(down_weight.astype(F32), axis=1)
    sums = ordered(sum_over(sum_over(sums, "c", 2), "yl", 2)).reshape(1, units)
    high = lax.reduce_precision(sums, 8, 7)
    middle = lax.reduce_precision(sums - high, 8, 7)
    lines = jnp.concatenate([high, middle, sums - high - middle]).astype(BF16)
    lines = jnp.pad(lines, ((0, EXTRA - 3), (0, width - units)))
    down = jnp.concatenate([ordered(down_weight), lines])
    down = lax.all_gather(down, "z", axis=0, tiled=False)

    mine = jnp.concatenate(
        [tokens] + [lax.ppermute(tokens, "x", shift(nx, -k)) for k in range(1, nx)]
    )
    mine = [mine] + [across(mine, k) for k in range(1, nyh * nyl)]
    other = [swap(m) for m in mine]

    hidden = hidden_units(mine, other, weights)
    far = lax.ppermute(hidden, "yl", flip(2, 1))
    hidden = [hidden, swap(hidden), far, swap(far)]
    unit_sums = jnp.concatenate([jnp.sum(h.astype(F32), axis=2) for h in hidden], axis=1)
    unit_sums = sum_over(unit_sums, "z", nz)[:, :, None]
    weight_sums = jnp.sum(down[:, units : units + 3, :units].astype(F32), axis=1)[:, :, None]

    targets = [(dy, dx) for dy in range(nyh) for dx in range(nx)]
    received = []
    for (dy, dx), piece in zip(
        targets, outputs(hidden, down, unit_sums, weight_sums, len(targets))
    ):
        perm = [(h * nx + i, (h ^ dy) * nx + (i + dx) % nx) for h in range(nyh) for i in range(nx)]
        if dx or dy:
            piece = lax.ppermute(piece, ("yh", "x"), perm)
        received.append(piece.astype(F32))
    mixed = sum(p[:rows] for p in received).astype(BF16)
    lines = sum(p[rows : rows + 2] for p in received)
    col_check = (lines[0] + lines[1]) / math.sqrt(total_tokens)
    row_check = 0.0
    for j, piece in enumerate(received):
        line = piece[rows + 2, j * rows : (j + 1) * rows] + piece[rows + 3, j * rows : (j + 1) * rows]
        row_check = row_check + line
    return (mixed, col_check, row_check / math.sqrt(model_width))


def solution(mesh):
    shape = mesh.shape
    sizes = (shape["dp"] // 2, 2, shape["row"] // 2, 2, shape["col"])
    fine = Mesh(np.asarray(mesh.devices).reshape(sizes), ("z", "yh", "yl", "c", "x"))
    batch = ("z", "yh", "x")
    return jax.shard_map(
        per_device,
        mesh=fine,
        in_specs=(P(batch, ROW), P(None, ROW, batch), P(batch, ROW)),
        out_specs=(P(batch, ROW), P(ROW), P(batch)),
        check_vma=False,
    )
```

```python
import functools
import math

import jax
import jax.numpy as jnp
import numpy as np
from jax import lax
from jax.experimental import pallas as pl
from jax.experimental.pallas import tpu as pltpu
from jax.sharding import Mesh, PartitionSpec as P

ROW = ("yl", "c")
EXTRA = 8
MINOR = (((1,), (1,)), ((), ()))
MAJOR = (((0,), (0,)), ((), ()))
F32 = jnp.float32
BF16 = jnp.bfloat16


def shift(n, step):
    return [(i, (i + step) % n) for i in range(n)]


def flip(n, mask):
    return [(i, i ^ mask) for i in range(n)]


def sum_over(value, axis, n):
    mask = 1
    while mask < n:
        value = value + lax.ppermute(value, axis, flip(n, mask))
        mask *= 2
    return value


def hidden_kernel(*refs):
    x_refs, weights_ref, out_ref = refs[:8], refs[8], refs[9]
    count, part = out_ref.shape[:2]
    depth = x_refs[0].shape[1]
    total = None
    for k in range(4):
        near = 4 * (k % 2) + k // 2
        x = jnp.concatenate([x_refs[near][...], x_refs[near + 2][...]])
        weights = weights_ref[:, pl.ds(k * depth, depth)]
        product = lax.dot_general(weights, x, MINOR, preferred_element_type=F32)
        total = product if total is None else total + product
    for j in range(count):
        gate = total[2 * part * j : 2 * part * j + part]
        up = total[2 * part * j + part : 2 * part * (j + 1)]
        out_ref[j] = (gate / (1.0 + jnp.exp(-gate)) * up).astype(BF16)


def hidden_units(mine, other, weights):
    count, units, wide = weights.shape
    total = 2 * mine[0].shape[0]
    return pl.pallas_call(
        hidden_kernel,
        out_shape=jax.ShapeDtypeStruct((count, units // 2, total), BF16),
        compiler_params=pltpu.CompilerParams(vmem_limit_bytes=56 << 20),
        cost_estimate=pl.CostEstimate(
            flops=2 * count * units * total * wide,
            transcendentals=count * units * total // 2,
            bytes_accessed=2 * (total + count * units) * wide,
        ),
        name="hidden",
    )(*mine, *other, weights.reshape(count * units, wide))


def output_kernel(pieces, blocks, *refs):
    hidden_refs, (down_ref, units_ref, weights_ref) = refs[:pieces], refs[pieces : pieces + 3]
    out_refs, (total, col, row) = refs[pieces + 3 : -3], refs[-3:]
    units = sum(r.shape[0] for r in hidden_refs)
    width = down_ref.shape[1]
    rows = total.shape[0] // blocks

    @pl.when(pl.program_id(0) == 0)
    def _():
        for sums in (total, col, row):
            sums[...] = jnp.zeros_like(sums)

    def fold(value):
        return jnp.sum(value.reshape(units // 8, 8, value.shape[1]), axis=0)

    hidden = jnp.concatenate([r[...].astype(F32) for r in hidden_refs])
    down = down_ref[pl.ds(0, units), :]
    total[...] += lax.dot_general(hidden.astype(BF16), down, MAJOR, preferred_element_type=F32)
    col[...] += fold(units_ref[...] * down.astype(F32))
    row[...] += fold(weights_ref[...] * hidden)

    @pl.when(pl.program_id(0) == pl.num_programs(0) - 1)
    def _():
        lines = []
        for sums in (col, row):
            value = jnp.sum(sums[...], axis=0, keepdims=True)
            high = value.astype(BF16).astype(F32)
            for line in (high, value - high):
                short = width - line.shape[1]
                if short:
                    line = jnp.concatenate([line, jnp.zeros((1, short), F32)], axis=1)
                lines.append(line)
        lines.append(jnp.zeros((EXTRA - len(lines), width), F32))
        lines = jnp.concatenate(lines).astype(BF16)
        for j in range(blocks):
            out_refs[j][pl.ds(0, rows), :] = total[pl.ds(j * rows, rows), :].astype(BF16)
            out_refs[j][pl.ds(rows, EXTRA), :] = lines


def outputs(hidden, down, unit_sums, weight_sums, blocks):
    steps, _, total = hidden[0].shape
    units = sum(h.shape[1] for h in hidden)
    width = down.shape[2]
    operands = [*hidden, down, unit_sums, weight_sums]
    piece = (total // blocks + EXTRA, width)
    return pl.pallas_call(
        functools.partial(output_kernel, len(hidden), blocks),
        out_shape=[jax.ShapeDtypeStruct(piece, BF16)] * blocks,
        grid=(steps,),
        in_specs=[pl.BlockSpec((None, *a.shape[1:]), lambda s: (s, 0, 0)) for a in operands],
        out_specs=[pl.BlockSpec(piece, lambda s: (0, 0))] * blocks,
        scratch_shapes=[
            pltpu.VMEM((total, width), F32),
            pltpu.VMEM((8, width), F32),
            pltpu.VMEM((8, total), F32),
        ],
        compiler_params=pltpu.CompilerParams(vmem_limit_bytes=48 << 20),
        cost_estimate=pl.CostEstimate(
            flops=2 * steps * units * total * width,
            transcendentals=0,
            bytes_accessed=2 * steps * units * (total + width) + 2 * total * width,
        ),
        name="outputs",
    )(*operands)


def per_device(tokens, gate_up, down_weight):
    rows, width = tokens.shape
    units = gate_up.shape[2]
    nz, nx, nyh, nyl, nrow = (lax.axis_size(a) for a in ("z", "x", "yh", "yl", ROW))
    part = units // nrow
    total_tokens = rows * nz * nx * nyh
    model_width = width * nrow
    own = lax.axis_index(ROW)

    def across(array, mask):
        return lax.ppermute(array, ("yh", "yl"), flip(nyh * nyl, mask))

    def swap(array):
        return lax.ppermute(array, "c", flip(2, 1))

    pieces = jnp.swapaxes(gate_up, 1, 2).reshape(2, nrow, part, width)
    weights = []
    for k in range(nrow):
        piece = lax.dynamic_index_in_dim(pieces, own ^ k, 1, keepdims=False)
        piece = piece.reshape(2 * part, width)
        weights.append(piece if k == 0 else lax.ppermute(piece, ROW, flip(nrow, k)))
    weights = lax.all_gather(jnp.concatenate(weights, axis=1), "z", axis=0, tiled=False)

    def ordered(array):
        array = array.reshape(nrow, part, -1)
        array = jnp.concatenate(
            [lax.dynamic_slice_in_dim(array, own ^ k, 1, 0) for k in range(nrow)]
        )
        return array.reshape(units, -1)

    sums = jnp.sum(down_weight.astype(F32), axis=1)
    sums = ordered(sum_over(sum_over(sums, "c", 2), "yl", 2)).reshape(1, units)
    high = lax.reduce_precision(sums, 8, 7)
    middle = lax.reduce_precision(sums - high, 8, 7)
    lines = jnp.concatenate([high, middle, sums - high - middle]).astype(BF16)
    lines = jnp.pad(lines, ((0, EXTRA - 3), (0, width - units)))
    down = jnp.concatenate([ordered(down_weight), lines])
    down = lax.all_gather(down, "z", axis=0, tiled=False)

    mine = jnp.concatenate(
        [tokens] + [lax.ppermute(tokens, "x", shift(nx, -k)) for k in range(1, nx)]
    )
    mine = [mine] + [across(mine, k) for k in range(1, nyh * nyl)]
    other = [swap(m) for m in mine]

    hidden = hidden_units(mine, other, weights)
    far = lax.ppermute(hidden, "yl", flip(2, 1))
    hidden = [hidden, swap(hidden), far, swap(far)]
    unit_sums = jnp.concatenate([jnp.sum(h.astype(F32), axis=2) for h in hidden], axis=1)
    unit_sums = sum_over(unit_sums, "z", nz)[:, :, None]
    weight_sums = jnp.sum(down[:, units : units + 3, :units].astype(F32), axis=1)[:, :, None]

    targets = [(dy, dx) for dy in range(nyh) for dx in range(nx)]
    far_first = sorted(range(len(targets)), key=lambda j: -2 * targets[j][0] - min(targets[j][1], nx - targets[j][1]))
    sent = outputs(hidden, down, unit_sums, weight_sums, len(targets))
    received = [None] * len(targets)
    for j in far_first:
        (dy, dx), piece = targets[j], sent[j]
        perm = [(h * nx + i, (h ^ dy) * nx + (i + dx) % nx) for h in range(nyh) for i in range(nx)]
        if dx or dy:
            piece = lax.ppermute(piece, ("yh", "x"), perm)
        received[j] = piece.astype(F32)
    mixed = sum(p[:rows] for p in received).astype(BF16)
    lines = sum(p[rows : rows + 2] for p in received)
    col_check = (lines[0] + lines[1]) / math.sqrt(total_tokens)
    row_check = 0.0
    for j, piece in enumerate(received):
        line = piece[rows + 2, j * rows : (j + 1) * rows] + piece[rows + 3, j * rows : (j + 1) * rows]
        row_check = row_check + line
    return (mixed, col_check, row_check / math.sqrt(model_width))


def solution(mesh):
    shape = mesh.shape
    sizes = (shape["dp"] // 2, 2, shape["row"] // 2, 2, shape["col"])
    fine = Mesh(np.asarray(mesh.devices).reshape(sizes), ("z", "yh", "yl", "c", "x"))
    batch = ("z", "yh", "x")
    return jax.shard_map(
        per_device,
        mesh=fine,
        in_specs=(P(batch, ROW), P(None, ROW, batch), P(batch, ROW)),
        out_specs=(P(batch, ROW), P(ROW), P(batch)),
        check_vma=False,
    )
```

```python
import functools
import math

import jax
import jax.numpy as jnp
import numpy as np
from jax import lax
from jax.experimental import pallas as pl
from jax.experimental.pallas import tpu as pltpu
from jax.sharding import Mesh, PartitionSpec as P

ROW = ("yl", "c")
EXTRA = 8
MINOR = (((1,), (1,)), ((), ()))
MAJOR = (((0,), (0,)), ((), ()))
F32 = jnp.float32
BF16 = jnp.bfloat16


def shift(n, step):
    return [(i, (i + step) % n) for i in range(n)]


def flip(n, mask):
    return [(i, i ^ mask) for i in range(n)]


def sum_over(value, axis, n):
    mask = 1
    while mask < n:
        value = value + lax.ppermute(value, axis, flip(n, mask))
        mask *= 2
    return value


def hidden_kernel(*refs):
    x_refs, weights_ref, out_ref = refs[:8], refs[8], refs[9]
    count, part = out_ref.shape[:2]
    depth = x_refs[0].shape[1]
    total = None
    for k in range(4):
        near = 4 * (k % 2) + k // 2
        x = jnp.concatenate([x_refs[near][...], x_refs[near + 2][...]])
        weights = weights_ref[:, pl.ds(k * depth, depth)]
        product = lax.dot_general(weights, x, MINOR, preferred_element_type=F32)
        total = product if total is None else total + product
    for j in range(count):
        gate = total[2 * part * j : 2 * part * j + part]
        up = total[2 * part * j + part : 2 * part * (j + 1)]
        out_ref[j] = (gate / (1.0 + jnp.exp(-gate)) * up).astype(BF16)


def hidden_units(mine, other, weights):
    count, units, wide = weights.shape
    total = 2 * mine[0].shape[0]
    return pl.pallas_call(
        hidden_kernel,
        out_shape=jax.ShapeDtypeStruct((count, units // 2, total), BF16),
        compiler_params=pltpu.CompilerParams(vmem_limit_bytes=56 << 20),
        cost_estimate=pl.CostEstimate(
            flops=2 * count * units * total * wide,
            transcendentals=count * units * total // 2,
            bytes_accessed=2 * (total + count * units) * wide,
        ),
        name="hidden",
    )(*mine, *other, weights.reshape(count * units, wide))


def output_kernel(pieces, blocks, *refs):
    hidden_refs, (down_ref, units_ref) = refs[:pieces], refs[pieces : pieces + 2]
    out_refs, (total, col, row) = refs[pieces + 2 : -3], refs[-3:]
    units = sum(r.shape[0] for r in hidden_refs)
    width = down_ref.shape[1]
    rows = total.shape[0] // blocks

    @pl.when(pl.program_id(0) == 0)
    def _():
        for sums in (total, col, row):
            sums[...] = jnp.zeros_like(sums)

    hidden = jnp.concatenate([r[...].astype(F32) for r in hidden_refs]).astype(BF16)
    down = down_ref[pl.ds(0, units), :]
    total[...] += lax.dot_general(hidden, down, MAJOR, preferred_element_type=F32)
    sums = units_ref[...]
    high = sums.astype(BF16).astype(F32)
    middle = (sums - high).astype(BF16).astype(F32)
    rest = jnp.zeros((EXTRA - 3, units), F32)
    terms = jnp.concatenate([high, middle, sums - high - middle, rest]).astype(BF16)
    col[...] += jnp.dot(terms, down, preferred_element_type=F32)
    weights = down_ref[pl.ds(units, EXTRA), pl.ds(0, units)]
    row[...] += jnp.dot(weights, hidden, preferred_element_type=F32)

    @pl.when(pl.program_id(0) == pl.num_programs(0) - 1)
    def _():
        lines = []
        for sums in (col, row):
            value = jnp.sum(sums[...], axis=0, keepdims=True)
            high = value.astype(BF16).astype(F32)
            for line in (high, value - high):
                short = width - line.shape[1]
                if short:
                    line = jnp.concatenate([line, jnp.zeros((1, short), F32)], axis=1)
                lines.append(line)
        lines.append(jnp.zeros((EXTRA - len(lines), width), F32))
        lines = jnp.concatenate(lines).astype(BF16)
        for j in range(blocks):
            out_refs[j][pl.ds(0, rows), :] = total[pl.ds(j * rows, rows), :].astype(BF16)
            out_refs[j][pl.ds(rows, EXTRA), :] = lines


def outputs(hidden, down, unit_sums, blocks):
    steps, _, total = hidden[0].shape
    units = sum(h.shape[1] for h in hidden)
    width = down.shape[2]
    operands = [*hidden, down, unit_sums]
    piece = (total // blocks + EXTRA, width)
    return pl.pallas_call(
        functools.partial(output_kernel, len(hidden), blocks),
        out_shape=[jax.ShapeDtypeStruct(piece, BF16)] * blocks,
        grid=(steps,),
        in_specs=[pl.BlockSpec((None, *a.shape[1:]), lambda s: (s, 0, 0)) for a in operands],
        out_specs=[pl.BlockSpec(piece, lambda s: (0, 0))] * blocks,
        scratch_shapes=[
            pltpu.VMEM((total, width), F32),
            pltpu.VMEM((8, width), F32),
            pltpu.VMEM((8, total), F32),
        ],
        compiler_params=pltpu.CompilerParams(vmem_limit_bytes=48 << 20),
        cost_estimate=pl.CostEstimate(
            flops=2 * steps * units * total * width,
            transcendentals=0,
            bytes_accessed=2 * steps * units * (total + width) + 2 * total * width,
        ),
        name="outputs",
    )(*operands)


def per_device(tokens, gate_up, down_weight):
    rows, width = tokens.shape
    units = gate_up.shape[2]
    nz, nx, nyh, nyl, nrow = (lax.axis_size(a) for a in ("z", "x", "yh", "yl", ROW))
    part = units // nrow
    total_tokens = rows * nz * nx * nyh
    model_width = width * nrow
    own = lax.axis_index(ROW)

    def across(array, mask):
        return lax.ppermute(array, ("yh", "yl"), flip(nyh * nyl, mask))

    def swap(array):
        return lax.ppermute(array, "c", flip(2, 1))

    pieces = jnp.swapaxes(gate_up, 1, 2).reshape(2, nrow, part, width)
    weights = []
    for k in range(nrow):
        piece = lax.dynamic_index_in_dim(pieces, own ^ k, 1, keepdims=False)
        piece = piece.reshape(2 * part, width)
        weights.append(piece if k == 0 else lax.ppermute(piece, ROW, flip(nrow, k)))
    weights = lax.all_gather(jnp.concatenate(weights, axis=1), "z", axis=0, tiled=False)

    def ordered(array):
        array = array.reshape(nrow, part, -1)
        array = jnp.concatenate(
            [lax.dynamic_slice_in_dim(array, own ^ k, 1, 0) for k in range(nrow)]
        )
        return array.reshape(units, -1)

    sums = jnp.sum(down_weight.astype(F32), axis=1)
    sums = ordered(sum_over(sum_over(sums, "c", 2), "yl", 2)).reshape(1, units)
    high = lax.reduce_precision(sums, 8, 7)
    middle = lax.reduce_precision(sums - high, 8, 7)
    lines = jnp.concatenate([high, middle, sums - high - middle]).astype(BF16)
    lines = jnp.pad(lines, ((0, EXTRA - 3), (0, width - units)))
    down = jnp.concatenate([ordered(down_weight), lines])
    down = lax.all_gather(down, "z", axis=0, tiled=False)

    mine = jnp.concatenate(
        [tokens] + [lax.ppermute(tokens, "x", shift(nx, -k)) for k in range(1, nx)]
    )
    mine = [mine] + [across(mine, k) for k in range(1, nyh * nyl)]
    other = [swap(m) for m in mine]

    hidden = hidden_units(mine, other, weights)
    far = lax.ppermute(hidden, "yl", flip(2, 1))
    hidden = [hidden, swap(hidden), far, swap(far)]
    unit_sums = jnp.concatenate([jnp.sum(h.astype(F32), axis=2) for h in hidden], axis=1)
    unit_sums = sum_over(unit_sums, "z", nz)[:, None, :]

    targets = [(dy, dx) for dy in range(nyh) for dx in range(nx)]
    far_first = sorted(
        range(len(targets)), key=lambda j: -2 * targets[j][0] - min(targets[j][1], nx - targets[j][1])
    )
    sent = outputs(hidden, down, unit_sums, len(targets))
    received = {}
    for j in far_first:
        (dy, dx), piece = targets[j], sent[j]
        perm = [(h * nx + i, (h ^ dy) * nx + (i + dx) % nx) for h in range(nyh) for i in range(nx)]
        if dx or dy:
            piece = lax.ppermute(piece, ("yh", "x"), perm)
        received[j] = piece.astype(F32)
    mixed = sum(p[:rows] for p in received.values()).astype(BF16)
    lines = sum(p[rows : rows + 2] for p in received.values())
    col_check = (lines[0] + lines[1]) / math.sqrt(total_tokens)
    row_check = 0.0
    for j, piece in received.items():
        line = piece[rows + 2, j * rows : (j + 1) * rows] + piece[rows + 3, j * rows : (j + 1) * rows]
        row_check = row_check + line
    return (mixed, col_check, row_check / math.sqrt(model_width))


def solution(mesh):
    shape = mesh.shape
    sizes = (shape["dp"] // 2, 2, shape["row"] // 2, 2, shape["col"])
    fine = Mesh(np.asarray(mesh.devices).reshape(sizes), ("z", "yh", "yl", "c", "x"))
    batch = ("z", "yh", "x")
    return jax.shard_map(
        per_device,
        mesh=fine,
        in_specs=(P(batch, ROW), P(None, ROW, batch), P(batch, ROW)),
        out_specs=(P(batch, ROW), P(ROW), P(batch)),
        check_vma=False,
    )
```

```python
import functools
import math

import jax
import jax.numpy as jnp
import numpy as np
from jax import lax
from jax.experimental import pallas as pl
from jax.experimental.pallas import tpu as pltpu
from jax.sharding import Mesh, PartitionSpec as P

ROW = ("yl", "c")
EXTRA = 8
GROUP = 8
MINOR = (((1,), (1,)), ((), ()))
MAJOR = (((0,), (0,)), ((), ()))
F32 = jnp.float32
BF16 = jnp.bfloat16


def shift(n, step):
    return [(i, (i + step) % n) for i in range(n)]


def flip(n, mask):
    return [(i, i ^ mask) for i in range(n)]


def sum_over(value, axis, n):
    mask = 1
    while mask < n:
        value = value + lax.ppermute(value, axis, flip(n, mask))
        mask *= 2
    return value


def gate(sent, waited=()):
    count = len(sent)
    anywhere = pl.BlockSpec(memory_space=pl.ANY)
    return pl.pallas_call(
        lambda *refs: None,
        out_shape=[jax.ShapeDtypeStruct(a.shape, a.dtype) for a in sent],
        in_specs=[anywhere] * (count + len(waited)),
        out_specs=[anywhere] * count,
        input_output_aliases={i: i for i in range(count)},
        name="gate",
    )(*sent, *waited)


def hidden_kernel(*refs):
    x_refs, weights_ref, out_ref = refs[:8], refs[8], refs[9]
    count, part = out_ref.shape[:2]
    depth = x_refs[0].shape[1]
    total = None
    for k in range(4):
        near = 4 * (k % 2) + k // 2
        x = jnp.concatenate([x_refs[near][...], x_refs[near + 2][...]])
        weights = weights_ref[:, pl.ds(k * depth, depth)]
        product = lax.dot_general(weights, x, MINOR, preferred_element_type=F32)
        total = product if total is None else total + product
    for j in range(count):
        gate = total[2 * part * j : 2 * part * j + part]
        up = total[2 * part * j + part : 2 * part * (j + 1)]
        out_ref[j] = (gate / (1.0 + jnp.exp(-gate)) * up).astype(BF16)


def hidden_units(mine, other, weights):
    count, units, wide = weights.shape
    total = 2 * mine[0].shape[0]
    return pl.pallas_call(
        hidden_kernel,
        out_shape=jax.ShapeDtypeStruct((count, units // 2, total), BF16),
        compiler_params=pltpu.CompilerParams(vmem_limit_bytes=56 << 20),
        cost_estimate=pl.CostEstimate(
            flops=2 * count * units * total * wide,
            transcendentals=count * units * total // 2,
            bytes_accessed=2 * (total + count * units) * wide,
        ),
        name="hidden",
    )(*mine, *other, weights.reshape(count * units, wide))


def output_kernel(pieces, blocks, *refs):
    hidden_refs, (down_ref, units_ref) = refs[:pieces], refs[pieces : pieces + 2]
    out_refs, (total, col, row) = refs[pieces + 2 : -3], refs[-3:]
    group, _, units = units_ref.shape
    width = down_ref.shape[2]
    rows = total.shape[0] // blocks

    @pl.when(pl.program_id(0) == 0)
    def _():
        for sums in (total, col, row):
            sums[...] = jnp.zeros_like(sums)

    hidden = jnp.concatenate([r[i] for i in range(group) for r in hidden_refs])
    down = jnp.concatenate([down_ref[i, pl.ds(0, units), :] for i in range(group)])
    total[...] += lax.dot_general(hidden, down, MAJOR, preferred_element_type=F32)
    for i in range(group):
        span = slice(i * units, (i + 1) * units)
        sums = units_ref[i]
        high = sums.astype(BF16).astype(F32)
        middle = (sums - high).astype(BF16).astype(F32)
        rest = jnp.zeros((EXTRA - 3, units), F32)
        terms = jnp.concatenate([high, middle, sums - high - middle, rest]).astype(BF16)
        col[...] += jnp.dot(terms, down[span], preferred_element_type=F32)
        weights = down_ref[i, pl.ds(units, EXTRA), pl.ds(0, units)]
        row[...] += jnp.dot(weights, hidden[span], preferred_element_type=F32)

    @pl.when(pl.program_id(0) == pl.num_programs(0) - 1)
    def _():
        lines = []
        for sums in (col, row):
            value = jnp.sum(sums[...], axis=0, keepdims=True)
            high = value.astype(BF16).astype(F32)
            for line in (high, value - high):
                short = width - line.shape[1]
                if short:
                    line = jnp.concatenate([line, jnp.zeros((1, short), F32)], axis=1)
                lines.append(line)
        lines.append(jnp.zeros((EXTRA - len(lines), width), F32))
        lines = jnp.concatenate(lines).astype(BF16)
        for j in range(blocks):
            out_refs[j][pl.ds(0, rows), :] = total[pl.ds(j * rows, rows), :].astype(BF16)
            out_refs[j][pl.ds(rows, EXTRA), :] = lines


def outputs(hidden, down, unit_sums, blocks):
    steps, _, total = hidden[0].shape
    units = sum(h.shape[1] for h in hidden)
    width = down.shape[2]
    operands = [*hidden, down, unit_sums]
    piece = (total // blocks + EXTRA, width)
    return pl.pallas_call(
        functools.partial(output_kernel, len(hidden), blocks),
        out_shape=[jax.ShapeDtypeStruct(piece, BF16)] * blocks,
        grid=(steps // math.gcd(steps, GROUP),),
        in_specs=[pl.BlockSpec((math.gcd(steps, GROUP), *a.shape[1:]), lambda s: (s, 0, 0)) for a in operands],
        out_specs=[pl.BlockSpec(piece, lambda s: (0, 0))] * blocks,
        scratch_shapes=[
            pltpu.VMEM((total, width), F32),
            pltpu.VMEM((8, width), F32),
            pltpu.VMEM((8, total), F32),
        ],
        compiler_params=pltpu.CompilerParams(vmem_limit_bytes=48 << 20),
        cost_estimate=pl.CostEstimate(
            flops=2 * steps * units * total * width,
            transcendentals=0,
            bytes_accessed=2 * steps * units * (total + width) + 2 * total * width,
        ),
        name="outputs",
    )(*operands)


def per_device(tokens, gate_up, down_weight):
    rows, width = tokens.shape
    units = gate_up.shape[2]
    nz, nx, nyh, nyl, nrow = (lax.axis_size(a) for a in ("z", "x", "yh", "yl", ROW))
    part = units // nrow
    total_tokens = rows * nz * nx * nyh
    model_width = width * nrow
    own = lax.axis_index(ROW)

    def across(array, mask):
        return lax.ppermute(array, ("yh", "yl"), flip(nyh * nyl, mask))

    def swap(array):
        return lax.ppermute(array, "c", flip(2, 1))

    pieces = jnp.swapaxes(gate_up, 1, 2).reshape(2, nrow, part, width)
    weights = []
    for k in range(nrow):
        piece = lax.dynamic_index_in_dim(pieces, own ^ k, 1, keepdims=False)
        piece = piece.reshape(2 * part, width)
        weights.append(piece if k == 0 else lax.ppermute(piece, ROW, flip(nrow, k)))
    weights = lax.all_gather(jnp.concatenate(weights, axis=1), "z", axis=0, tiled=False)

    def ordered(array):
        array = array.reshape(nrow, part, -1)
        array = jnp.concatenate(
            [lax.dynamic_slice_in_dim(array, own ^ k, 1, 0) for k in range(nrow)]
        )
        return array.reshape(units, -1)

    sums = jnp.sum(down_weight.astype(F32), axis=1)
    sums = ordered(sum_over(sum_over(sums, "c", 2), "yl", 2)).reshape(1, units)
    high = lax.reduce_precision(sums, 8, 7)
    middle = lax.reduce_precision(sums - high, 8, 7)
    lines = jnp.concatenate([high, middle, sums - high - middle]).astype(BF16)
    lines = jnp.pad(lines, ((0, EXTRA - 3), (0, width - units)))
    down = jnp.concatenate([ordered(down_weight), lines])
    down = lax.all_gather(down, "z", axis=0, tiled=False)

    mine = jnp.concatenate(
        [tokens] + [lax.ppermute(tokens, "x", shift(nx, -k)) for k in range(1, nx)]
    )
    mine = [mine] + [across(mine, k) for k in range(1, nyh * nyl)]
    other = [swap(m) for m in mine]

    hidden = hidden_units(mine, other, weights)
    unit_sums = sum_over(jnp.sum(hidden.astype(F32), axis=2), "z", nz)
    far = lax.ppermute(hidden, "yl", flip(2, 1))
    (far,) = gate([far], [unit_sums])
    hidden = [hidden, swap(hidden), far, swap(far)]
    far = lax.ppermute(unit_sums, "yl", flip(2, 1))
    unit_sums = [unit_sums, swap(unit_sums), far, swap(far)]
    unit_sums = jnp.concatenate(unit_sums, axis=1)[:, None, :]

    targets = [(dy, dx) for dy in range(nyh) for dx in range(nx)]
    far_first = sorted(
        range(len(targets)), key=lambda j: -2 * targets[j][0] - min(targets[j][1], nx - targets[j][1])
    )
    sent = outputs(hidden, down, unit_sums, len(targets))
    received = {}
    for j in far_first:
        (dy, dx), piece = targets[j], sent[j]
        perm = [(h * nx + i, (h ^ dy) * nx + (i + dx) % nx) for h in range(nyh) for i in range(nx)]
        if dx or dy:
            piece = lax.ppermute(piece, ("yh", "x"), perm)
        received[j] = piece.astype(F32)
    mixed = sum(p[:rows] for p in received.values()).astype(BF16)
    lines = sum(p[rows : rows + 2] for p in received.values())
    col_check = (lines[0] + lines[1]) / math.sqrt(total_tokens)
    row_check = 0.0
    for j, piece in received.items():
        line = piece[rows + 2, j * rows : (j + 1) * rows] + piece[rows + 3, j * rows : (j + 1) * rows]
        row_check = row_check + line
    return (mixed, col_check, row_check / math.sqrt(model_width))


def solution(mesh):
    shape = mesh.shape
    sizes = (shape["dp"] // 2, 2, shape["row"] // 2, 2, shape["col"])
    fine = Mesh(np.asarray(mesh.devices).reshape(sizes), ("z", "yh", "yl", "c", "x"))
    batch = ("z", "yh", "x")
    return jax.shard_map(
        per_device,
        mesh=fine,
        in_specs=(P(batch, ROW), P(None, ROW, batch), P(batch, ROW)),
        out_specs=(P(batch, ROW), P(ROW), P(batch)),
        check_vma=False,
    )
```

```python
import functools
import math

import jax
import jax.numpy as jnp
import numpy as np
from jax import lax
from jax.experimental import pallas as pl
from jax.experimental.pallas import tpu as pltpu
from jax.sharding import Mesh, PartitionSpec as P

ROW = ("yl", "c")
EXTRA = 8
GROUP = 8
MINOR = (((1,), (1,)), ((), ()))
MAJOR = (((0,), (0,)), ((), ()))
F32 = jnp.float32
BF16 = jnp.bfloat16


def shift(n, step):
    return [(i, (i + step) % n) for i in range(n)]


def flip(n, mask):
    return [(i, i ^ mask) for i in range(n)]


def sum_over(value, axis, n):
    mask = 1
    while mask < n:
        value = value + lax.ppermute(value, axis, flip(n, mask))
        mask *= 2
    return value


def gate(sent, waited=()):
    count = len(sent)
    anywhere = pl.BlockSpec(memory_space=pl.ANY)
    return pl.pallas_call(
        lambda *refs: None,
        out_shape=[jax.ShapeDtypeStruct(a.shape, a.dtype) for a in sent],
        in_specs=[anywhere] * (count + len(waited)),
        out_specs=[anywhere] * count,
        input_output_aliases={i: i for i in range(count)},
        name="gate",
    )(*sent, *waited)


def hidden_kernel(*refs):
    x_refs, weights_ref, out_ref = refs[:8], refs[8], refs[9]
    count, part = out_ref.shape[:2]
    depth = x_refs[0].shape[1]
    total = None
    for k in range(4):
        near = 4 * (k % 2) + k // 2
        x = jnp.concatenate([x_refs[near][...], x_refs[near + 2][...]])
        weights = weights_ref[:, pl.ds(k * depth, depth)]
        product = lax.dot_general(weights, x, MINOR, preferred_element_type=F32)
        total = product if total is None else total + product
    for j in range(count):
        gate = total[2 * part * j : 2 * part * j + part]
        up = total[2 * part * j + part : 2 * part * (j + 1)]
        out_ref[j] = (gate / (1.0 + jnp.exp(-gate)) * up).astype(BF16)


def hidden_units(mine, other, weights):
    count, units, wide = weights.shape
    total = 2 * mine[0].shape[0]
    return pl.pallas_call(
        hidden_kernel,
        out_shape=jax.ShapeDtypeStruct((count, units // 2, total), BF16),
        compiler_params=pltpu.CompilerParams(vmem_limit_bytes=56 << 20),
        cost_estimate=pl.CostEstimate(
            flops=2 * count * units * total * wide,
            transcendentals=count * units * total // 2,
            bytes_accessed=2 * (total + count * units) * wide,
        ),
        name="hidden",
    )(*mine, *other, weights.reshape(count * units, wide))


def output_kernel(pieces, blocks, *refs):
    hidden_refs, (down_ref, units_ref) = refs[:pieces], refs[pieces : pieces + 2]
    out_refs, (total, col, row) = refs[pieces + 2 : -3], refs[-3:]
    group, _, units = units_ref.shape
    width = down_ref.shape[2]
    rows = total.shape[0] // blocks

    @pl.when(pl.program_id(0) == 0)
    def _():
        for sums in (total, col, row):
            sums[...] = jnp.zeros_like(sums)

    hidden = jnp.concatenate([r[i] for i in range(group) for r in hidden_refs])
    down = jnp.concatenate([down_ref[i, pl.ds(0, units), :] for i in range(group)])
    total[...] += lax.dot_general(hidden, down, MAJOR, preferred_element_type=F32)
    for i in range(group):
        span = slice(i * units, (i + 1) * units)
        sums = units_ref[i]
        high = sums.astype(BF16).astype(F32)
        middle = (sums - high).astype(BF16).astype(F32)
        rest = jnp.zeros((EXTRA - 3, units), F32)
        terms = jnp.concatenate([high, middle, sums - high - middle, rest]).astype(BF16)
        col[...] += jnp.dot(terms, down[span], preferred_element_type=F32)
        weights = down_ref[i, pl.ds(units, EXTRA), pl.ds(0, units)]
        row[...] += jnp.dot(weights, hidden[span], preferred_element_type=F32)

    @pl.when(pl.program_id(0) == pl.num_programs(0) - 1)
    def _():
        lines = []
        for sums in (col, row):
            value = jnp.sum(sums[...], axis=0, keepdims=True)
            high = value.astype(BF16).astype(F32)
            for line in (high, value - high):
                short = width - line.shape[1]
                if short:
                    line = jnp.concatenate([line, jnp.zeros((1, short), F32)], axis=1)
                lines.append(line)
        lines.append(jnp.zeros((EXTRA - len(lines), width), F32))
        lines = jnp.concatenate(lines).astype(BF16)
        for j in range(blocks):
            out_refs[j][pl.ds(0, rows), :] = total[pl.ds(j * rows, rows), :].astype(BF16)
            out_refs[j][pl.ds(rows, EXTRA), :] = lines


def outputs(hidden, down, unit_sums, blocks):
    steps, _, total = hidden[0].shape
    units = sum(h.shape[1] for h in hidden)
    width = down.shape[2]
    operands = [*hidden, down, unit_sums]
    piece = (total // blocks + EXTRA, width)
    return pl.pallas_call(
        functools.partial(output_kernel, len(hidden), blocks),
        out_shape=[jax.ShapeDtypeStruct(piece, BF16)] * blocks,
        grid=(steps // math.gcd(steps, GROUP),),
        in_specs=[pl.BlockSpec((math.gcd(steps, GROUP), *a.shape[1:]), lambda s: (s, 0, 0)) for a in operands],
        out_specs=[pl.BlockSpec(piece, lambda s: (0, 0))] * blocks,
        scratch_shapes=[
            pltpu.VMEM((total, width), F32),
            pltpu.VMEM((8, width), F32),
            pltpu.VMEM((8, total), F32),
        ],
        compiler_params=pltpu.CompilerParams(vmem_limit_bytes=48 << 20),
        cost_estimate=pl.CostEstimate(
            flops=2 * steps * units * total * width,
            transcendentals=0,
            bytes_accessed=2 * steps * units * (total + width) + 2 * total * width,
        ),
        name="outputs",
    )(*operands)


def per_device(tokens, gate_up, down_weight):
    rows, width = tokens.shape
    units = gate_up.shape[2]
    nz, nx, nyh, nyl, nrow = (lax.axis_size(a) for a in ("z", "x", "yh", "yl", ROW))
    part = units // nrow
    total_tokens = rows * nz * nx * nyh
    model_width = width * nrow
    own = lax.axis_index(ROW)

    def across(array, mask):
        return lax.ppermute(array, ("yh", "yl"), flip(nyh * nyl, mask))

    def swap(array):
        return lax.ppermute(array, "c", flip(2, 1))

    pieces = jnp.swapaxes(gate_up, 1, 2).reshape(2, nrow, part, width)
    weights = []
    for k in range(nrow):
        piece = lax.dynamic_index_in_dim(pieces, own ^ k, 1, keepdims=False)
        piece = piece.reshape(2 * part, width)
        weights.append(piece if k == 0 else lax.ppermute(piece, ROW, flip(nrow, k)))
    weights = lax.all_gather(jnp.concatenate(weights, axis=1), "z", axis=0, tiled=False)

    def ordered(array):
        array = array.reshape(nrow, part, -1)
        array = jnp.concatenate(
            [lax.dynamic_slice_in_dim(array, own ^ k, 1, 0) for k in range(nrow)]
        )
        return array.reshape(units, -1)

    sums = jnp.sum(down_weight.astype(F32), axis=1)
    sums = ordered(sum_over(sum_over(sums, "c", 2), "yl", 2)).reshape(1, units)
    high = lax.reduce_precision(sums, 8, 7)
    middle = lax.reduce_precision(sums - high, 8, 7)
    lines = jnp.concatenate([high, middle, sums - high - middle]).astype(BF16)
    lines = jnp.pad(lines, ((0, EXTRA - 3), (0, width - units)))
    down = jnp.concatenate([ordered(down_weight), lines])
    down = lax.all_gather(down, "z", axis=0, tiled=False)

    mine = jnp.concatenate(
        [tokens] + [lax.ppermute(tokens, "x", shift(nx, -k)) for k in range(1, nx)]
    )
    mine = [mine] + [across(mine, k) for k in range(1, nyh * nyl)]
    other = [swap(m) for m in mine]

    hidden = hidden_units(mine, other, weights)
    unit_sums = sum_over(jnp.sum(hidden.astype(F32), axis=2), "z", nz)
    far = lax.ppermute(hidden, "yl", flip(2, 1))
    (far,) = gate([far], [unit_sums])
    hidden = [hidden, swap(hidden), far, swap(far)]
    far = lax.ppermute(unit_sums, "yl", flip(2, 1))
    unit_sums = [unit_sums, swap(unit_sums), far, swap(far)]
    unit_sums = jnp.concatenate(unit_sums, axis=1)[:, None, :]

    targets = [(dy, dx) for dy in range(nyh) for dx in range(nx)]
    leave = [targets.index(t) for t in ((1, 1), (0, 2), (1, 3), (1, 2), (1, 0), (0, 1), (0, 3), (0, 0))]
    sent = outputs(hidden, down, unit_sums, len(targets))
    received = {}
    for j in leave:
        (dy, dx), piece = targets[j], sent[j]
        perm = [(h * nx + i, (h ^ dy) * nx + (i + dx) % nx) for h in range(nyh) for i in range(nx)]
        if dx or dy:
            piece = lax.ppermute(piece, ("yh", "x"), perm)
        received[j] = piece.astype(F32)
    mixed = sum(p[:rows] for p in received.values()).astype(BF16)
    lines = sum(p[rows : rows + 2] for p in received.values())
    col_check = (lines[0] + lines[1]) / math.sqrt(total_tokens)
    row_check = 0.0
    for j, piece in received.items():
        line = piece[rows + 2, j * rows : (j + 1) * rows] + piece[rows + 3, j * rows : (j + 1) * rows]
        row_check = row_check + line
    return (mixed, col_check, row_check / math.sqrt(model_width))


def solution(mesh):
    shape = mesh.shape
    sizes = (shape["dp"] // 2, 2, shape["row"] // 2, 2, shape["col"])
    fine = Mesh(np.asarray(mesh.devices).reshape(sizes), ("z", "yh", "yl", "c", "x"))
    batch = ("z", "yh", "x")
    return jax.shard_map(
        per_device,
        mesh=fine,
        in_specs=(P(batch, ROW), P(None, ROW, batch), P(batch, ROW)),
        out_specs=(P(batch, ROW), P(ROW), P(batch)),
        check_vma=False,
    )
```

```python
import functools
import math

import jax
import jax.numpy as jnp
import numpy as np
from jax import lax
from jax.experimental import pallas as pl
from jax.experimental.pallas import tpu as pltpu
from jax.sharding import Mesh, PartitionSpec as P

ROW = ("yl", "c")
EXTRA = 8
GROUP = 8
MINOR = (((1,), (1,)), ((), ()))
MAJOR = (((0,), (0,)), ((), ()))
F32 = jnp.float32
BF16 = jnp.bfloat16


def shift(n, step):
    return [(i, (i + step) % n) for i in range(n)]


def flip(n, mask):
    return [(i, i ^ mask) for i in range(n)]


def sum_over(value, axis, n):
    mask = 1
    while mask < n:
        value = value + lax.ppermute(value, axis, flip(n, mask))
        mask *= 2
    return value


def gate(sent, waited=()):
    count = len(sent)
    anywhere = pl.BlockSpec(memory_space=pl.ANY)
    return pl.pallas_call(
        lambda *refs: None,
        out_shape=[jax.ShapeDtypeStruct(a.shape, a.dtype) for a in sent],
        in_specs=[anywhere] * (count + len(waited)),
        out_specs=[anywhere] * count,
        input_output_aliases={i: i for i in range(count)},
        name="gate",
    )(*sent, *waited)


def hidden_kernel(*refs):
    x_refs, weights_ref, out_ref = refs[:8], refs[8], refs[9]
    count, part = out_ref.shape[:2]
    depth = x_refs[0].shape[1]
    total = None
    for k in range(4):
        near = 4 * (k % 2) + k // 2
        x = jnp.concatenate([x_refs[near][...], x_refs[near + 2][...]])
        weights = weights_ref[:, pl.ds(k * depth, depth)]
        product = lax.dot_general(weights, x, MINOR, preferred_element_type=F32)
        total = product if total is None else total + product
    for j in range(count):
        gate = total[2 * part * j : 2 * part * j + part]
        up = total[2 * part * j + part : 2 * part * (j + 1)]
        out_ref[j] = (gate / (1.0 + jnp.exp(-gate)) * up).astype(BF16)


def hidden_units(mine, other, weights):
    count, units, wide = weights.shape
    total = 2 * mine[0].shape[0]
    return pl.pallas_call(
        hidden_kernel,
        out_shape=jax.ShapeDtypeStruct((count, units // 2, total), BF16),
        compiler_params=pltpu.CompilerParams(vmem_limit_bytes=56 << 20),
        cost_estimate=pl.CostEstimate(
            flops=2 * count * units * total * wide,
            transcendentals=count * units * total // 2,
            bytes_accessed=2 * (total + count * units) * wide,
        ),
        name="hidden",
    )(*mine, *other, weights.reshape(count * units, wide))


def output_kernel(pieces, blocks, *refs):
    hidden_refs, (down_ref, units_ref) = refs[:pieces], refs[pieces : pieces + 2]
    out_refs, (total, col, row) = refs[pieces + 2 : -3], refs[-3:]
    group, _, units = units_ref.shape
    width = down_ref.shape[2]
    rows = total.shape[0] // blocks

    @pl.when(pl.program_id(0) == 0)
    def _():
        for sums in (total, col, row):
            sums[...] = jnp.zeros_like(sums)

    hidden = jnp.concatenate([r[i] for i in range(group) for r in hidden_refs])
    down = jnp.concatenate([down_ref[i, pl.ds(0, units), :] for i in range(group)])
    total[...] += lax.dot_general(hidden, down, MAJOR, preferred_element_type=F32)
    for i in range(group):
        span = slice(i * units, (i + 1) * units)
        sums = units_ref[i]
        high = sums.astype(BF16).astype(F32)
        middle = (sums - high).astype(BF16).astype(F32)
        rest = jnp.zeros((EXTRA - 3, units), F32)
        terms = jnp.concatenate([high, middle, sums - high - middle, rest]).astype(BF16)
        col[...] += jnp.dot(terms, down[span], preferred_element_type=F32)
        weights = down_ref[i, pl.ds(units, EXTRA), pl.ds(0, units)]
        row[...] += jnp.dot(weights, hidden[span], preferred_element_type=F32)

    @pl.when(pl.program_id(0) == pl.num_programs(0) - 1)
    def _():
        lines = []
        for sums in (col, row):
            value = jnp.sum(sums[...], axis=0, keepdims=True)
            high = value.astype(BF16).astype(F32)
            for line in (high, value - high):
                short = width - line.shape[1]
                if short:
                    line = jnp.concatenate([line, jnp.zeros((1, short), F32)], axis=1)
                lines.append(line)
        lines.append(jnp.zeros((EXTRA - len(lines), width), F32))
        lines = jnp.concatenate(lines).astype(BF16)
        for j in range(blocks):
            out_refs[j][pl.ds(0, rows), :] = total[pl.ds(j * rows, rows), :].astype(BF16)
            out_refs[j][pl.ds(rows, EXTRA), :] = lines


def outputs(hidden, down, unit_sums, blocks):
    steps, _, total = hidden[0].shape
    units = sum(h.shape[1] for h in hidden)
    width = down.shape[2]
    operands = [*hidden, down, unit_sums]
    piece = (total // blocks + EXTRA, width)
    return pl.pallas_call(
        functools.partial(output_kernel, len(hidden), blocks),
        out_shape=[jax.ShapeDtypeStruct(piece, BF16)] * blocks,
        grid=(steps // math.gcd(steps, GROUP),),
        in_specs=[pl.BlockSpec((math.gcd(steps, GROUP), *a.shape[1:]), lambda s: (s, 0, 0)) for a in operands],
        out_specs=[pl.BlockSpec(piece, lambda s: (0, 0))] * blocks,
        scratch_shapes=[
            pltpu.VMEM((total, width), F32),
            pltpu.VMEM((8, width), F32),
            pltpu.VMEM((8, total), F32),
        ],
        compiler_params=pltpu.CompilerParams(vmem_limit_bytes=48 << 20),
        cost_estimate=pl.CostEstimate(
            flops=2 * steps * units * total * width,
            transcendentals=0,
            bytes_accessed=2 * steps * units * (total + width) + 2 * total * width,
        ),
        name="outputs",
    )(*operands)


def per_device(tokens, gate_up, down_weight):
    rows, width = tokens.shape
    units = gate_up.shape[2]
    nz, nx, nyh, nyl, nrow = (lax.axis_size(a) for a in ("z", "x", "yh", "yl", ROW))
    part = units // nrow
    total_tokens = rows * nz * nx * nyh
    model_width = width * nrow
    own = lax.axis_index(ROW)

    def across(array, mask):
        return lax.ppermute(array, ("yh", "yl"), flip(nyh * nyl, mask))

    def swap(array):
        return lax.ppermute(array, "c", flip(2, 1))

    pieces = jnp.swapaxes(gate_up, 1, 2).reshape(2, nrow, part, width)
    weights = []
    for k in range(nrow):
        piece = lax.dynamic_index_in_dim(pieces, own ^ k, 1, keepdims=False)
        piece = piece.reshape(2 * part, width)
        weights.append(piece if k == 0 else lax.ppermute(piece, ROW, flip(nrow, k)))
    weights = lax.all_gather(jnp.concatenate(weights, axis=1), "z", axis=0, tiled=False)

    def ordered(array):
        array = array.reshape(nrow, part, -1)
        array = jnp.concatenate(
            [lax.dynamic_slice_in_dim(array, own ^ k, 1, 0) for k in range(nrow)]
        )
        return array.reshape(units, -1)

    sums = jnp.sum(down_weight.astype(F32), axis=1)
    sums = ordered(sum_over(sum_over(sums, "c", 2), "yl", 2)).reshape(1, units)
    high = lax.reduce_precision(sums, 8, 7)
    middle = lax.reduce_precision(sums - high, 8, 7)
    lines = jnp.concatenate([high, middle, sums - high - middle]).astype(BF16)
    lines = jnp.pad(lines, ((0, EXTRA - 3), (0, width - units)))
    down = jnp.concatenate([ordered(down_weight), lines])
    down = lax.all_gather(down, "z", axis=0, tiled=False)

    mine = jnp.concatenate(
        [tokens] + [lax.ppermute(tokens, "x", shift(nx, -k)) for k in range(1, nx)]
    )
    mine = [mine] + [across(mine, k) for k in range(1, nyh * nyl)]
    other = [swap(m) for m in mine]

    hidden = hidden_units(mine, other, weights)
    unit_sums = sum_over(jnp.sum(hidden.astype(F32), axis=2), "z", nz)
    far = lax.ppermute(hidden, "yl", flip(2, 1))
    (passed,) = gate([far], [unit_sums])
    hidden = [hidden, swap(hidden), far, swap(passed)]
    far = lax.ppermute(unit_sums, "yl", flip(2, 1))
    unit_sums = [unit_sums, swap(unit_sums), far, swap(far)]
    corners = [h[0, :8, :128] for h in (hidden[1], hidden[3])]
    (unit_sums,) = gate([jnp.concatenate(unit_sums, axis=1)], corners)
    unit_sums = unit_sums[:, None, :]

    targets = [(dy, dx) for dy in range(nyh) for dx in range(nx)]
    leave = [targets.index(t) for t in ((1, 1), (0, 2), (1, 3), (1, 2), (1, 0), (0, 1), (0, 3), (0, 0))]
    sent = outputs(hidden, down, unit_sums, len(targets))
    received = {}
    for j in leave:
        (dy, dx), piece = targets[j], sent[j]
        perm = [(h * nx + i, (h ^ dy) * nx + (i + dx) % nx) for h in range(nyh) for i in range(nx)]
        if dx or dy:
            piece = lax.ppermute(piece, ("yh", "x"), perm)
        received[j] = piece.astype(F32)
    mixed = sum(p[:rows] for p in received.values()).astype(BF16)
    lines = sum(p[rows : rows + 2] for p in received.values())
    col_check = (lines[0] + lines[1]) / math.sqrt(total_tokens)
    row_check = 0.0
    for j, piece in received.items():
        line = piece[rows + 2, j * rows : (j + 1) * rows] + piece[rows + 3, j * rows : (j + 1) * rows]
        row_check = row_check + line
    return (mixed, col_check, row_check / math.sqrt(model_width))


def solution(mesh):
    shape = mesh.shape
    sizes = (shape["dp"] // 2, 2, shape["row"] // 2, 2, shape["col"])
    fine = Mesh(np.asarray(mesh.devices).reshape(sizes), ("z", "yh", "yl", "c", "x"))
    batch = ("z", "yh", "x")
    return jax.shard_map(
        per_device,
        mesh=fine,
        in_specs=(P(batch, ROW), P(None, ROW, batch), P(batch, ROW)),
        out_specs=(P(batch, ROW), P(ROW), P(batch)),
        check_vma=False,
    )
```

```python
import functools
import math

import jax
import jax.numpy as jnp
import numpy as np
from jax import lax
from jax.experimental import pallas as pl
from jax.experimental.pallas import tpu as pltpu
from jax.sharding import Mesh, PartitionSpec as P

ROW = ("yl", "c")
EXTRA = 8
GROUP = 8
MINOR = (((1,), (1,)), ((), ()))
MAJOR = (((0,), (0,)), ((), ()))
F32 = jnp.float32
BF16 = jnp.bfloat16


def shift(n, step):
    return [(i, (i + step) % n) for i in range(n)]


def flip(n, mask):
    return [(i, i ^ mask) for i in range(n)]


def sum_over(value, axis, n):
    mask = 1
    while mask < n:
        value = value + lax.ppermute(value, axis, flip(n, mask))
        mask *= 2
    return value


def gate(sent, waited=()):
    count = len(sent)
    anywhere = pl.BlockSpec(memory_space=pl.ANY)
    return pl.pallas_call(
        lambda *refs: None,
        out_shape=[jax.ShapeDtypeStruct(a.shape, a.dtype) for a in sent],
        in_specs=[anywhere] * (count + len(waited)),
        out_specs=[anywhere] * count,
        input_output_aliases={i: i for i in range(count)},
        name="gate",
    )(*sent, *waited)


def hidden_kernel(*refs):
    x_refs, weights_ref, out_ref = refs[:8], refs[8], refs[-1]
    count, part = out_ref.shape[:2]
    depth = x_refs[0].shape[1]
    total = None
    for k in range(4):
        near = 4 * (k % 2) + k // 2
        x = jnp.concatenate([x_refs[near][...], x_refs[near + 2][...]])
        weights = weights_ref[:, pl.ds(k * depth, depth)]
        product = lax.dot_general(weights, x, MINOR, preferred_element_type=F32)
        total = product if total is None else total + product
    for j in range(count):
        gate = total[2 * part * j : 2 * part * j + part]
        up = total[2 * part * j + part : 2 * part * (j + 1)]
        out_ref[j] = (gate / (1.0 + jnp.exp(-gate)) * up).astype(BF16)


def hidden_units(mine, other, weights, waited):
    count, units, wide = weights.shape
    total = 2 * mine[0].shape[0]
    return pl.pallas_call(
        hidden_kernel,
        out_shape=jax.ShapeDtypeStruct((count, units // 2, total), BF16),
        compiler_params=pltpu.CompilerParams(vmem_limit_bytes=56 << 20),
        cost_estimate=pl.CostEstimate(
            flops=2 * count * units * total * wide,
            transcendentals=count * units * total // 2,
            bytes_accessed=2 * (total + count * units) * wide,
        ),
        name="hidden",
    )(*mine, *other, weights.reshape(count * units, wide), waited)


def output_kernel(pieces, blocks, *refs):
    hidden_refs, (down_ref, units_ref, weights_ref) = refs[:pieces], refs[pieces : pieces + 3]
    out_refs, (total, col, row) = refs[pieces + 3 : -3], refs[-3:]
    group, _, units = units_ref.shape
    width = down_ref.shape[2]
    rows = total.shape[0] // blocks

    @pl.when(pl.program_id(0) == 0)
    def _():
        for sums in (total, col, row):
            sums[...] = jnp.zeros_like(sums)

    hidden = jnp.concatenate([r[i] for i in range(group) for r in hidden_refs])
    down = jnp.concatenate([down_ref[i, pl.ds(0, units), :] for i in range(group)])
    total[...] += lax.dot_general(hidden, down, MAJOR, preferred_element_type=F32)
    def terms(sums):
        high = sums.astype(BF16).astype(F32)
        middle = (sums - high).astype(BF16).astype(F32)
        rest = jnp.zeros((EXTRA - 3, units), F32)
        return jnp.concatenate([high, middle, sums - high - middle, rest]).astype(BF16)

    for i in range(group):
        span = slice(i * units, (i + 1) * units)
        col[...] += jnp.dot(terms(units_ref[i]), down[span], preferred_element_type=F32)
        row[...] += jnp.dot(terms(weights_ref[i]), hidden[span], preferred_element_type=F32)

    @pl.when(pl.program_id(0) == pl.num_programs(0) - 1)
    def _():
        lines = []
        for sums in (col, row):
            value = jnp.sum(sums[...], axis=0, keepdims=True)
            high = value.astype(BF16).astype(F32)
            for line in (high, value - high):
                short = width - line.shape[1]
                if short:
                    line = jnp.concatenate([line, jnp.zeros((1, short), F32)], axis=1)
                lines.append(line)
        lines.append(jnp.zeros((EXTRA - len(lines), width), F32))
        lines = jnp.concatenate(lines).astype(BF16)
        for j in range(blocks):
            out_refs[j][pl.ds(0, rows), :] = total[pl.ds(j * rows, rows), :].astype(BF16)
            out_refs[j][pl.ds(rows, EXTRA), :] = lines


def outputs(hidden, down, unit_sums, weight_sums, blocks):
    steps, _, total = hidden[0].shape
    units = sum(h.shape[1] for h in hidden)
    width = down.shape[2]
    operands = [*hidden, down, unit_sums, weight_sums]
    piece = (total // blocks + EXTRA, width)
    return pl.pallas_call(
        functools.partial(output_kernel, len(hidden), blocks),
        out_shape=[jax.ShapeDtypeStruct(piece, BF16)] * blocks,
        grid=(steps // math.gcd(steps, GROUP),),
        in_specs=[pl.BlockSpec((math.gcd(steps, GROUP), *a.shape[1:]), lambda s: (s, 0, 0)) for a in operands],
        out_specs=[pl.BlockSpec(piece, lambda s: (0, 0))] * blocks,
        scratch_shapes=[
            pltpu.VMEM((total, width), F32),
            pltpu.VMEM((8, width), F32),
            pltpu.VMEM((8, total), F32),
        ],
        compiler_params=pltpu.CompilerParams(vmem_limit_bytes=48 << 20),
        cost_estimate=pl.CostEstimate(
            flops=2 * steps * units * total * width,
            transcendentals=0,
            bytes_accessed=2 * steps * units * (total + width) + 2 * total * width,
        ),
        name="outputs",
    )(*operands)


def per_device(tokens, gate_up, down_weight):
    rows, width = tokens.shape
    units = gate_up.shape[2]
    nz, nx, nyh, nyl, nrow = (lax.axis_size(a) for a in ("z", "x", "yh", "yl", ROW))
    part = units // nrow
    total_tokens = rows * nz * nx * nyh
    model_width = width * nrow
    own = lax.axis_index(ROW)

    def across(array, mask):
        return lax.ppermute(array, ("yh", "yl"), flip(nyh * nyl, mask))

    def swap(array):
        return lax.ppermute(array, "c", flip(2, 1))

    pieces = jnp.swapaxes(gate_up, 1, 2).reshape(2, nrow, part, width)
    weights = []
    for k in range(nrow):
        piece = lax.dynamic_index_in_dim(pieces, own ^ k, 1, keepdims=False)
        piece = piece.reshape(2 * part, width)
        weights.append(piece if k == 0 else lax.ppermute(piece, ROW, flip(nrow, k)))
    weights = lax.all_gather(jnp.concatenate(weights, axis=1), "z", axis=0, tiled=False)

    def ordered(array):
        array = array.reshape(nrow, part, -1)
        array = jnp.concatenate(
            [lax.dynamic_slice_in_dim(array, own ^ k, 1, 0) for k in range(nrow)]
        )
        return array.reshape(units, -1)

    sums = jnp.sum(down_weight.astype(F32), axis=1)
    sums = ordered(sum_over(sum_over(sums, "c", 2), "yl", 2)).reshape(1, units)
    here = (jnp.arange(nz) == lax.axis_index("z"))[:, None]
    weight_sums = sum_over(jnp.where(here, sums, 0.0), "z", nz)
    down = ordered(down_weight)
    down = lax.all_gather(down, "z", axis=0, tiled=False)

    mine = jnp.concatenate(
        [tokens] + [lax.ppermute(tokens, "x", shift(nx, -k)) for k in range(1, nx)]
    )
    mine = [mine] + [across(mine, k) for k in range(1, nyh * nyl)]
    other = [swap(m) for m in mine]

    hidden = hidden_units(mine, other, weights, weight_sums)
    unit_sums = sum_over(jnp.sum(hidden.astype(F32), axis=2), "z", nz)
    far = lax.ppermute(hidden, "yl", flip(2, 1))
    (passed,) = gate([far], [unit_sums])
    hidden = [hidden, swap(hidden), far, swap(passed)]
    far = lax.ppermute(unit_sums, "yl", flip(2, 1))
    unit_sums = [unit_sums, swap(unit_sums), far, swap(far)]
    corners = [h[0, :8, :128] for h in (hidden[1], hidden[3])]
    unit_sums, weight_sums = gate([jnp.concatenate(unit_sums, axis=1), weight_sums], corners)
    unit_sums, weight_sums = unit_sums[:, None, :], weight_sums[:, None, :]

    targets = [(dy, dx) for dy in range(nyh) for dx in range(nx)]
    leave = [targets.index(t) for t in ((1, 1), (0, 2), (1, 3), (1, 2), (1, 0), (0, 1), (0, 3), (0, 0))]
    sent = outputs(hidden, down, unit_sums, weight_sums, len(targets))
    received = {}
    for j in leave:
        (dy, dx), piece = targets[j], sent[j]
        perm = [(h * nx + i, (h ^ dy) * nx + (i + dx) % nx) for h in range(nyh) for i in range(nx)]
        if dx or dy:
            piece = lax.ppermute(piece, ("yh", "x"), perm)
        received[j] = piece.astype(F32)
    mixed = sum(p[:rows] for p in received.values()).astype(BF16)
    lines = sum(p[rows : rows + 2] for p in received.values())
    col_check = (lines[0] + lines[1]) / math.sqrt(total_tokens)
    row_check = 0.0
    for j, piece in received.items():
        line = piece[rows + 2, j * rows : (j + 1) * rows] + piece[rows + 3, j * rows : (j + 1) * rows]
        row_check = row_check + line
    return (mixed, col_check, row_check / math.sqrt(model_width))


def solution(mesh):
    shape = mesh.shape
    sizes = (shape["dp"] // 2, 2, shape["row"] // 2, 2, shape["col"])
    fine = Mesh(np.asarray(mesh.devices).reshape(sizes), ("z", "yh", "yl", "c", "x"))
    batch = ("z", "yh", "x")
    return jax.shard_map(
        per_device,
        mesh=fine,
        in_specs=(P(batch, ROW), P(None, ROW, batch), P(batch, ROW)),
        out_specs=(P(batch, ROW), P(ROW), P(batch)),
        check_vma=False,
    )
```
